32 devices in a mesh: row: 8 (over z, core), col: 4 (over y, x).
Axes of the slice: x: 2, y: 2, z: 4, core: 2. Of those that a mesh axis runs over, the one named last changes fastest.
Arguments:
- amplitudes: bfloat16 [256, 4, 16384], P('col', None, 'row'), may hold values from -6 to 6
- integrals: bfloat16 [4, 16384, 16384], P(None, 'row', 'col'), may hold values from -0.046875 to 0.046875
- block_sizes: int32 [4], replicated, may hold values from 8192 to 16384, as said below
Outputs:
- ladder: float32 [256, 4, 16384], P('row', None, 'col')
The draws below stay inside these ranges and needn't reach their ends.
Inputs may be any that keep to these rules, and one draw needn't show every extreme that they name: Each irrep block uses its first block_sizes[h] pairs; in every draw some block uses all 16384.
All inputs are finite; a program needn't handle non-finite values.
Results may differ from the reference program's by a relative error of at most 0.0003.
Values may be sent and summed in bfloat16 or wider, within the bound.
A program may use at most 128 MiB of HBM per device.

```python
import jax
import jax.numpy as jnp

NIRR = 4
P_SIZE = 16384
NPAIR = 256


def draw_block_sizes(key, part):
    first, second = jax.random.split(jax.random.fold_in(key, 7))
    sizes = jax.random.randint(first, (NIRR,), P_SIZE // 2, P_SIZE + 1)
    chosen = jax.random.randint(second, (), 0, NIRR)
    full = jnp.full((NIRR,), P_SIZE, jnp.int32)
    return jnp.where(jnp.arange(NIRR) == chosen, full, sizes).astype(jnp.int32)


def levels(stream_key, dims, shards, low, largest):
    gain, own = 1.0, jax.random.fold_in(stream_key, 6)
    for dim, blocks in shards:
        draws = jnp.exp(jax.random.uniform(jax.random.fold_in(own, dim), (blocks,), jnp.float32, low / len(shards), largest / len(shards)))
        gain = gain * jnp.repeat(draws, dims[dim] // blocks).reshape([-1 if axis == dim else 1 for axis in range(len(dims))])
    return gain


def scatter_about(stream_key, shape, spread, limit, shards=(), kind=jnp.bfloat16):
    level = levels(stream_key, shape, shards, -0.22, 0.18) if shards else 1.0
    result = jax.random.normal(stream_key, shape, jnp.float32) * spread * level
    return jnp.minimum(jnp.maximum(result, -limit), limit).astype(kind)


def setup_inputs(seed: int = 0) -> dict:
    key_of = jax.random.split(jax.random.key(seed), 4)
    amplitudes = scatter_about(key_of[0], (NPAIR, NIRR, P_SIZE), 1.0, 6.0, ((0, 4), (2, 8)))
    integrals = scatter_about(key_of[1], (NIRR, P_SIZE, P_SIZE), P_SIZE ** -0.5, 0.046875, ((1, 8), (2, 4)))
    block_sizes = draw_block_sizes(jax.random.fold_in(key_of[3], 71), 0)
    return dict(amplitudes=amplitudes, integrals=integrals, block_sizes=block_sizes)


def reference(amplitudes, integrals, block_sizes):
    columns = jnp.arange(P_SIZE, dtype=jnp.int32)
    blocks = []
    for irrep in range(NIRR):
        live = columns < block_sizes[irrep]
        masked = jnp.where(live[None, :], amplitudes[:, irrep, :], jnp.zeros((), amplitudes.dtype))
        total = jnp.dot(masked, integrals[irrep], preferred_element_type=jnp.float32)
        blocks.append(jnp.where(live[None, :], total, jnp.zeros((), jnp.float32)))
    return jnp.stack(blocks, 1)
```

```python
import functools

import jax
import jax.numpy as jnp
from jax import lax
from jax.experimental import pallas as pl
from jax.experimental.pallas import tpu as pltpu
from jax.sharding import PartitionSpec as P

CORES = 2
SLOTS = 3
TILE = 256
LAG = 2
TOP = 32766.0
TINY = 1e-30


def kernel(chips, cols, steps, chunk, sizes, amp, integ, out, gathered, masked, panel, part, peer, stage, inbox,
           scale_out, scale_in, own_sem, gather_send, gather_recv, panel_sem, peer_send, peer_recv,
           stage_send, inbox_recv, scale_send, scale_recv):
    row, col = lax.axis_index("row"), lax.axis_index("col")
    z, core = row // CORES, row % CORES
    blocks, share, span = amp.shape
    pairs = stage.shape[2]
    per_block = steps // blocks
    width = chunk * per_block
    mate = z * CORES + 1 - core

    def send(src, dst, send_sem, recv_sem, to_row, to_col):
        return pltpu.make_async_remote_copy(
            src_ref=src, dst_ref=dst, send_sem=send_sem, recv_sem=recv_sem,
            device_id={"row": to_row, "col": to_col}, device_id_type=pl.DeviceIdType.MESH)

    def panel_copy(t):
        lanes = pl.ds(pl.multiple_of((t % per_block) * chunk, chunk), chunk)
        slot = t % SLOTS
        return pltpu.make_async_copy(integ.at[t // per_block, :, lanes], panel.at[slot], panel_sem.at[slot])

    def gather_copy(h, k):
        return send(amp.at[h], gathered.at[h, col], gather_send.at[h, k], gather_recv.at[h, col],
                    row, (col + k) % cols)

    def gather_wait(h, k):
        source = (col + k) % cols
        send(amp.at[h], gathered.at[h, source], gather_send.at[h, k], gather_recv.at[h, source], row, source).wait_recv()

    def own_copy(h):
        return pltpu.make_async_copy(amp.at[h], gathered.at[h, col], own_sem.at[h])

    def peer_copy(t):
        return send(part.at[t, :, 1 - core], peer.at[t], peer_send.at[t], peer_recv.at[t], mate, col)

    def data_copy(t, d, way, to_row):
        slot = d + 1 - way
        return send(stage.at[t, d], inbox.at[t, slot], stage_send.at[t, d], inbox_recv.at[t, slot], to_row, col)

    def scale_copy(t, way, to_row):
        return send(scale_out.at[way, t], scale_in.at[way, t], scale_send.at[way, t], scale_recv.at[way, t], to_row, col)

    def loop(low, high, body):
        lax.fori_loop(low, high, lambda i, c: (body(i), c)[1], 0)

    for t in range(min(SLOTS, steps)):
        panel_copy(t).start()
    loop(0, blocks, lambda h: own_copy(h).start())

    barrier = pltpu.get_barrier_semaphore()

    def greet(to_row, to_col):
        pl.semaphore_signal(barrier, inc=1, device_id={"row": to_row, "col": to_col},
                            device_id_type=pl.DeviceIdType.MESH)

    loop(1, cols, lambda k: greet(row, (col + k) % cols))
    greet(mate, col)

    @pl.when(z > 0)
    def _():
        greet(row - CORES, col)

    @pl.when(z < chips - 1)
    def _():
        greet(row + CORES, col)

    pl.semaphore_wait(barrier, cols + jnp.where(z > 0, 1, 0) + jnp.where(z < chips - 1, 1, 0))

    loop(0, blocks, lambda h: loop(1, cols, lambda k: gather_copy(h, k).start()))

    def compute(t):
        h = t // per_block

        @pl.when(t % per_block == 0)
        def _():
            own_copy(h).wait()
            loop(1, cols, lambda k: gather_wait(h, k))
            index = row * span + lax.broadcasted_iota(jnp.int32, (share, span), 1)
            live = index < sizes[h]

            def fill(c):
                values = jnp.where(live, gathered[h, c].astype(jnp.float32), 0.0)
                masked[pl.ds(pl.multiple_of(c * share, share), share), :] = values.astype(masked.dtype)

            loop(0, cols, fill)

        panel_copy(t).wait()
        slot = t % SLOTS

        def tile(n):
            lanes = pl.ds(pl.multiple_of(n * TILE, TILE), TILE)
            value = jnp.dot(masked[...], panel[slot, :, lanes], preferred_element_type=jnp.float32)
            part[t, :, :, :, lanes] = value.reshape(chips, CORES, pairs, TILE)

        loop(0, chunk // TILE, tile)
        peer_copy(t).start()

        @pl.when(t + SLOTS < steps)
        def _():
            panel_copy(t + SLOTS).start()

    def combine(t):
        peer_copy(t).wait_recv()

        def add(d):
            part[t, d, core] = part[t, d, core] + peer[t, d]

        loop(0, chips, add)

    def relay(t, way):
        up = way == 0
        has_source = z > 0 if up else z < chips - 1
        has_target = z < chips - 1 if up else z > 0
        to_row = row + CORES if up else row - CORES
        first, last = (z + 1, chips) if up else (0, z)

        @pl.when(has_source)
        def _():
            scale_copy(t, way, row).wait_recv()
            factor = scale_in[way, t]

            def take(d):
                data_copy(t, d, way, row).wait_recv()
                part[t, d, core] = part[t, d, core] + inbox[t, d + 1 - way].astype(jnp.int32).astype(jnp.float32) * factor

            loop(*((z, chips) if up else (0, z + 1)), take)

        @pl.when(has_target)
        def _():
            largest = lax.fori_loop(
                first, last,
                lambda d, m: jnp.maximum(m, jnp.max(jnp.abs(part[t, d, core]), axis=0, keepdims=True)),
                jnp.full((1, chunk), TINY, jnp.float32))
            scale_out[way, t] = largest * (1.0 / TOP)
            scale_copy(t, way, to_row).start()
            inverse = TOP / largest

            def put(d):
                stage[t, d] = jnp.round(part[t, d, core] * inverse).astype(jnp.int32).astype(jnp.int16)
                data_copy(t, d, way, to_row).start()

            loop(0, last - first, (lambda j: put(last - 1 - j)) if up else put)

    def finish(t):
        h = t // per_block
        low = (t % per_block) * chunk
        index = col * width + low + lax.broadcasted_iota(jnp.int32, (pairs, chunk), 1)
        out[h, :, pl.ds(pl.multiple_of(low, chunk), chunk)] = jnp.where(index < sizes[h], part[t, z, core], 0.0)

    def at(t, body):
        @pl.when(jnp.logical_and(t >= 0, t < steps))
        def _():
            body(t)

    up_lag = 1 + LAG * z
    down_lag = 1 + LAG * (chips - 1 - z)
    end_lag = 1 + LAG * chips

    def step(i):
        at(i, compute)
        at(i - 1, combine)
        at(i - up_lag, lambda t: relay(t, 0))
        at(i - down_lag, lambda t: relay(t, 1))
        at(i - end_lag, finish)

    loop(0, steps + end_lag, step)

    loop(0, blocks, lambda h: loop(1, cols, lambda k: gather_copy(h, k).wait_send()))

    def drain(t):
        peer_copy(t).wait_send()

        @pl.when(z < chips - 1)
        def _():
            scale_copy(t, 0, row).wait_send()
            loop(z + 1, chips, lambda d: data_copy(t, d, 0, row).wait_send())

        @pl.when(z > 0)
        def _():
            scale_copy(t, 1, row).wait_send()
            loop(0, z, lambda d: data_copy(t, d, 1, row).wait_send())

    loop(0, steps, drain)


def body(chips, cols, amplitudes, integrals, block_sizes):
    share, blocks, span = amplitudes.shape
    width = integrals.shape[2]
    chunk = min(1024, width)
    steps = blocks * (width // chunk)
    total = share * cols
    pairs = total // (chips * CORES)
    dma = pltpu.SemaphoreType.DMA
    result = pl.pallas_call(
        functools.partial(kernel, chips, cols, steps, chunk),
        out_shape=jax.ShapeDtypeStruct((blocks, pairs, width), jnp.float32),
        in_specs=[
            pl.BlockSpec(memory_space=pltpu.SMEM),
            pl.BlockSpec(memory_space=pl.ANY),
            pl.BlockSpec(memory_space=pl.ANY),
        ],
        out_specs=pl.BlockSpec(memory_space=pltpu.VMEM),
        scratch_shapes=[
            pltpu.VMEM((blocks, cols, share, span), amplitudes.dtype),
            pltpu.VMEM((total, span), amplitudes.dtype),
            pltpu.VMEM((SLOTS, span, chunk), integrals.dtype),
            pltpu.VMEM((steps, chips, CORES, pairs, chunk), jnp.float32),
            pltpu.VMEM((steps, chips, pairs, chunk), jnp.float32),
            pltpu.VMEM((steps, chips, pairs, chunk), jnp.int16),
            pltpu.VMEM((steps, chips + 1, pairs, chunk), jnp.int16),
            pltpu.VMEM((2, steps, 1, chunk), jnp.float32),
            pltpu.VMEM((2, steps, 1, chunk), jnp.float32),
            dma((blocks,)),
            dma((blocks, cols)),
            dma((blocks, cols)),
            dma((SLOTS,)),
            dma((steps,)),
            dma((steps,)),
            dma((steps, chips)),
            dma((steps, chips + 1)),
            dma((2, steps)),
            dma((2, steps)),
        ],
        compiler_params=pltpu.CompilerParams(
            collective_id=0, has_side_effects=True, vmem_limit_bytes=63 * 2**20
        ),
        name="ladder",
    )(block_sizes, amplitudes.transpose(1, 0, 2), integrals)
    return result.transpose(1, 0, 2)


def solution(mesh):
    placed = (P("col", None, "row"), P(None, "row", "col"), P())
    return jax.shard_map(
        functools.partial(body, mesh.shape["row"] // CORES, mesh.shape["col"]),
        mesh=mesh, in_specs=placed, out_specs=P("row", None, "col"), check_vma=False,
    )
```

```python
import functools

import jax
import jax.numpy as jnp
from jax import lax
from jax.experimental import pallas as pl
from jax.experimental.pallas import tpu as pltpu
from jax.sharding import PartitionSpec as P

CORES = 2
SLOTS = 4
TILE = 256
LAG = 2
TOP = 32766.0
TINY = 1e-30


def kernel(chips, cols, steps, chunk, sizes, amp, integ, out, gathered, masked, panel, part, peer, stage, inbox,
           scale_out, scale_in, own_sem, gather_send, gather_recv, panel_sem, peer_send, peer_recv,
           stage_send, inbox_recv, scale_send, scale_recv):
    row, col = lax.axis_index("row"), lax.axis_index("col")
    z, core = row // CORES, row % CORES
    blocks, _, pairs, span = amp.shape
    per_block = steps // blocks
    early = min(per_block, SLOTS)
    width = chunk * per_block
    mate = z * CORES + 1 - core

    def send(src, dst, send_sem, recv_sem, to_row, to_col):
        return pltpu.make_async_remote_copy(
            src_ref=src, dst_ref=dst, send_sem=send_sem, recv_sem=recv_sem,
            device_id={"row": to_row, "col": to_col}, device_id_type=pl.DeviceIdType.MESH)

    def panel_copy(t):
        lanes = pl.ds(pl.multiple_of((t % per_block) * chunk, chunk), chunk)
        slot = t % SLOTS
        return pltpu.make_async_copy(integ.at[t // per_block, :, lanes], panel.at[slot], panel_sem.at[slot])

    def gather_copy(h, q, k):
        return send(amp.at[h, q], gathered.at[h, q, col], gather_send.at[h, q, k], gather_recv.at[h, q, col],
                    row, (col + k) % cols)

    def gather_wait(h, q, k):
        source = (col + k) % cols
        send(amp.at[h, q], gathered.at[h, q, source], gather_send.at[h, q, k], gather_recv.at[h, q, source],
             row, source).wait_recv()

    def own_copy(h, q):
        return pltpu.make_async_copy(amp.at[h, q], gathered.at[h, q, col], own_sem.at[h, q])

    def peer_copy(t):
        return send(part.at[t, 1 - core], peer.at[t], peer_send.at[t], peer_recv.at[t], mate, col)

    def data_copy(t, d, way, to_row):
        slot = d + 1 - way
        return send(stage.at[t, d], inbox.at[t, slot], stage_send.at[t, d], inbox_recv.at[t, slot], to_row, col)

    def scale_copy(t, way, to_row):
        return send(scale_out.at[way, t], scale_in.at[way, t], scale_send.at[way, t], scale_recv.at[way, t], to_row, col)

    def loop(low, high, body):
        lax.fori_loop(low, high, lambda i, c: (body(i), c)[1], 0)

    for t in range(min(SLOTS, steps)):
        panel_copy(t).start()
    loop(0, blocks, lambda h: loop(0, CORES, lambda q: own_copy(h, q).start()))

    barrier = pltpu.get_barrier_semaphore()

    def greet(to_row, to_col):
        pl.semaphore_signal(barrier, inc=1, device_id={"row": to_row, "col": to_col},
                            device_id_type=pl.DeviceIdType.MESH)

    loop(1, cols, lambda k: greet(row, (col + k) % cols))
    greet(mate, col)

    @pl.when(z > 0)
    def _():
        greet(row - CORES, col)

    @pl.when(z < chips - 1)
    def _():
        greet(row + CORES, col)

    pl.semaphore_wait(barrier, cols + jnp.where(z > 0, 1, 0) + jnp.where(z < chips - 1, 1, 0))

    loop(0, blocks, lambda h: loop(0, CORES, lambda q: loop(1, cols, lambda k: gather_copy(h, q, k).start())))

    def prepare(h, q):
        own_copy(h, q).wait()
        loop(1, cols, lambda k: gather_wait(h, q, k))
        index = row * span + lax.broadcasted_iota(jnp.int32, (pairs, span), 1)
        live = index < sizes[h]

        def fill(c):
            values = jnp.where(live, gathered[h, q, c].astype(jnp.float32), 0.0)
            masked[q, pl.ds(pl.multiple_of(c * pairs, pairs), pairs), :] = values.astype(masked.dtype)

        loop(0, cols, fill)

    def next_panel(t):
        @pl.when(t + SLOTS < steps)
        def _():
            panel_copy(t + SLOTS).start()

    def half(t, q):
        @pl.when(t == 0)
        def _():
            prepare(0, q)

        @pl.when(q == 0)
        def _():
            panel_copy(t).wait()

        slot = t % SLOTS

        def tile(n):
            lanes = pl.ds(pl.multiple_of(n * TILE, TILE), TILE)
            value = jnp.dot(masked[q], panel[slot, :, lanes], preferred_element_type=jnp.float32)
            part[t, q, :, :, lanes] = value.reshape(chips, pairs, TILE)

        loop(0, chunk // TILE, tile)

        @pl.when(core != q)
        def _():
            peer_copy(t).start()

        @pl.when(q == 1)
        def _():
            next_panel(t)

    def full(t):
        @pl.when(t % per_block == 0)
        def _():
            loop(0, CORES, lambda q: prepare(t // per_block, q))

        panel_copy(t).wait()
        slot = t % SLOTS

        def tile(n):
            lanes = pl.ds(pl.multiple_of(n * TILE, TILE), TILE)
            left = masked[...].reshape(CORES * chips * pairs, span)
            value = jnp.dot(left, panel[slot, :, lanes], preferred_element_type=jnp.float32)
            part[t, :, :, :, lanes] = value.reshape(CORES, chips, pairs, TILE)

        loop(0, chunk // TILE, tile)
        peer_copy(t).start()
        next_panel(t)

    def combine(t):
        peer_copy(t).wait_recv()

        def add(d):
            part[t, core, d] = part[t, core, d] + peer[t, d]

        loop(0, chips, add)

    def relay(t, way):
        up = way == 0
        has_source = z > 0 if up else z < chips - 1
        has_target = z < chips - 1 if up else z > 0
        to_row = row + CORES if up else row - CORES
        first, last = (z + 1, chips) if up else (0, z)

        @pl.when(has_source)
        def _():
            scale_copy(t, way, row).wait_recv()
            factor = scale_in[way, t]

            def take(d):
                data_copy(t, d, way, row).wait_recv()
                part[t, core, d] = part[t, core, d] + inbox[t, d + 1 - way].astype(jnp.int32).astype(jnp.float32) * factor

            loop(*((z, chips) if up else (0, z + 1)), take)

        @pl.when(has_target)
        def _():
            largest = lax.fori_loop(
                first, last,
                lambda d, m: jnp.maximum(m, jnp.max(jnp.abs(part[t, core, d]), axis=0, keepdims=True)),
                jnp.full((1, chunk), TINY, jnp.float32))
            scale_out[way, t] = largest * (1.0 / TOP)
            scale_copy(t, way, to_row).start()
            inverse = TOP / largest

            def put(d):
                stage[t, d] = jnp.round(part[t, core, d] * inverse).astype(jnp.int32).astype(jnp.int16)
                data_copy(t, d, way, to_row).start()

            loop(0, last - first, (lambda j: put(last - 1 - j)) if up else put)

    def finish(t):
        h = t // per_block
        low = (t % per_block) * chunk
        index = col * width + low + lax.broadcasted_iota(jnp.int32, (pairs, chunk), 1)
        out[h, :, pl.ds(pl.multiple_of(low, chunk), chunk)] = jnp.where(index < sizes[h], part[t, core, z], 0.0)

    def when(condition, body, *args):
        @pl.when(condition)
        def _():
            body(*args)

    def at(j, body):
        ahead = jnp.logical_and(core == 0, j < early)
        t = jnp.where(ahead, j, jnp.where(jnp.logical_and(core == 0, j < 2 * early), -1, j - early))
        when(jnp.logical_and(t >= 0, t < steps), body, t)

    up_lag = 1 + LAG * z
    down_lag = 1 + LAG * (chips - 1 - z)
    end_lag = 1 + LAG * chips

    def step(i):
        when(jnp.logical_and(i < 2 * early, i != early), lambda: half(i % early, i // early))
        when(jnp.logical_and(i >= 2 * early, i < steps + early), lambda: full(i - early))
        at(i - 1, combine)
        at(i - up_lag, lambda t: relay(t, 0))
        at(i - down_lag, lambda t: relay(t, 1))
        at(i - end_lag, finish)
        when(i == early, lambda: half(0, 1))

    loop(0, steps + early + end_lag, step)

    loop(0, blocks, lambda h: loop(0, CORES, lambda q: loop(1, cols, lambda k: gather_copy(h, q, k).wait_send())))

    def drain(t):
        peer_copy(t).wait_send()

        @pl.when(z < chips - 1)
        def _():
            scale_copy(t, 0, row).wait_send()
            loop(z + 1, chips, lambda d: data_copy(t, d, 0, row).wait_send())

        @pl.when(z > 0)
        def _():
            scale_copy(t, 1, row).wait_send()
            loop(0, z, lambda d: data_copy(t, d, 1, row).wait_send())

    loop(0, steps, drain)


def body(chips, cols, amplitudes, integrals, block_sizes):
    share, blocks, span = amplitudes.shape
    width = integrals.shape[2]
    chunk = min(1024, width)
    steps = blocks * (width // chunk)
    total = share * cols
    pairs = total // (chips * CORES)
    assert share == CORES * pairs and chips == cols
    dma = pltpu.SemaphoreType.DMA
    result = pl.pallas_call(
        functools.partial(kernel, chips, cols, steps, chunk),
        out_shape=jax.ShapeDtypeStruct((blocks, pairs, width), jnp.float32),
        in_specs=[
            pl.BlockSpec(memory_space=pltpu.SMEM),
            pl.BlockSpec(memory_space=pl.ANY),
            pl.BlockSpec(memory_space=pl.ANY),
        ],
        out_specs=pl.BlockSpec(memory_space=pltpu.VMEM),
        scratch_shapes=[
            pltpu.VMEM((blocks, CORES, cols, pairs, span), amplitudes.dtype),
            pltpu.VMEM((CORES, chips * pairs, span), amplitudes.dtype),
            pltpu.VMEM((SLOTS, span, chunk), integrals.dtype),
            pltpu.VMEM((steps, CORES, chips, pairs, chunk), jnp.float32),
            pltpu.VMEM((steps, chips, pairs, chunk), jnp.float32),
            pltpu.VMEM((steps, chips, pairs, chunk), jnp.int16),
            pltpu.VMEM((steps, chips + 1, pairs, chunk), jnp.int16),
            pltpu.VMEM((2, steps, 1, chunk), jnp.float32),
            pltpu.VMEM((2, steps, 1, chunk), jnp.float32),
            dma((blocks, CORES)),
            dma((blocks, CORES, cols)),
            dma((blocks, CORES, cols)),
            dma((SLOTS,)),
            dma((steps,)),
            dma((steps,)),
            dma((steps, chips)),
            dma((steps, chips + 1)),
            dma((2, steps)),
            dma((2, steps)),
        ],
        compiler_params=pltpu.CompilerParams(
            collective_id=0, has_side_effects=True, vmem_limit_bytes=63 * 2**20
        ),
        name="ladder",
    )(block_sizes, amplitudes.reshape(CORES, pairs, blocks, span).transpose(2, 0, 1, 3), integrals)
    return result.transpose(1, 0, 2)


def solution(mesh):
    placed = (P("col", None, "row"), P(None, "row", "col"), P())
    return jax.shard_map(
        functools.partial(body, mesh.shape["row"] // CORES, mesh.shape["col"]),
        mesh=mesh, in_specs=placed, out_specs=P("row", None, "col"), check_vma=False,
    )
```
